32 devices in a mesh: groups: 2 (over y), row: 4 (over z), col: 2 (over x), rep: 2 (over core).
Axes of the slice: x: 2, y: 2, z: 4, core: 2. Of those that a mesh axis runs over, the one named last changes fastest.
Arguments:
- left_panel: float32 [192512, 2048], P(('groups', 'row', 'col', 'rep')), parts along dimension 0, may hold values from -0.02734375 to 0.02734375
- earlier: float32 [192512, 256], P(('groups', 'row', 'col', 'rep')), parts along dimension 0, may hold values from -6 to 6
- diag_block: float32 [4096, 2048], P(('groups', 'col'), 'row'), parts along dimension 0, as said below
- chosen: int32 [512], P(('groups', 'row', 'rep')), parts along dimension 0, may hold values from 0 to 2047
Outputs:
- marginal: float32 [4096, 256], P(('groups', 'col'), ('row', 'rep')), parts along dimension 0
- updated: float32 [192512, 256], P(('groups', 'row', 'col', 'rep')), parts along dimension 0
The draws below stay inside these ranges and needn't reach their ends.
There are 2 independent parts, one for each index of `groups`. The reference program is written for one: setup_inputs(seed, part) draws one part's arguments, and reference() takes and returns one part's arrays. A program takes and returns all parts, laid end to end along the dimension named above; each array names one. Nothing has to cross between parts.
Inputs may be any that keep to these rules, and one draw needn't show every extreme that they name: diag_block is lower triangular with diagonal entries from 1 to 2.
All inputs are finite; a program needn't handle non-finite values.
Results may differ from the reference program's by a relative error of at most 0.00029.
Values sent between devices are 32-bit elements; how exact they have to be, the bound alone decides.
No kernel may reach another device: no remote copies, remote signals or barrier semaphores. Data moves between devices by JAX's collectives and lax.ppermute only.
A program may use at most 192 MiB of HBM per device.

```python
import math
import jax
import jax.numpy as jnp
from jax import lax

SLAB = 2048
RHS = 256
LEFT = 96256


def draw_diag_block(key, part):
    first_key, second_key = jax.random.split(jax.random.fold_in(key, 11))
    spread = 2.0 / math.sqrt(SLAB)
    offdiag = jax.random.normal(first_key, (SLAB, SLAB), jnp.float32) * spread
    diagonal = jnp.exp(jax.random.uniform(second_key, (SLAB,), jnp.float32, 0.0, math.log(2.0)))
    indices = jnp.arange(SLAB)
    below = indices[:, None] > indices[None, :]
    on_diag = indices[:, None] == indices[None, :]
    result = jnp.where(below, offdiag, 0.0)
    result = jnp.where(on_diag, diagonal[:, None] * jnp.ones((1, SLAB), jnp.float32), result)
    return result.astype(jnp.float32)


def with_ends(values, key, low, top_value):
    index_at = [jax.random.randint(jax.random.fold_in(key, axis), (), 0, length) for axis, length in enumerate(values.shape)]
    widest = values.shape.index(max(values.shape))
    beside = index_at[:widest] + [(index_at[widest] + 1) % values.shape[widest]] + index_at[widest + 1:]
    return values.at[tuple(index_at)].set(low).at[tuple(beside)].set(top_value)


def strengthened(values, key, source, target, shards_of, factor):
    def block_of(position):
        return (jnp.arange(values.shape[position]) // (values.shape[position] // shards_of)).reshape((-1,) + (1,) * (values.ndim - 1 - position))

    first = jax.random.permutation(key, shards_of)[block_of(target)]
    other_side = (block_of(target) + shards_of // 2) % shards_of
    return jnp.where((block_of(source) == first) | (block_of(source) == other_side), factor * values, values)


def levels(own_key, extent, shards, low, high):
    def one(dim, parts):
        steps = jax.random.uniform(jax.random.fold_in(jax.random.fold_in(own_key, 6), dim), (parts,), jnp.float32, low / len(shards), high / len(shards))
        return jnp.repeat(jnp.exp(steps), extent[dim] // parts).reshape((-1,) + (1,) * (len(extent) - dim - 1))

    gain = one(*shards[0])
    for cut in shards[1:]:
        gain = gain * one(*cut)
    return gain


def noise(rng, extent, scale, limit, pieces=(), held_as=jnp.bfloat16):
    values = scale * jax.random.normal(rng, extent, jnp.float32)
    if pieces:
        values = values * levels(rng, extent, pieces, -0.22, 0.18)
    return jnp.clip(values, -limit, limit).astype(held_as)


def gaussian_with(key, shape, width, limit, shards, heavy, held_as=jnp.bfloat16):
    array = width * jax.random.normal(key, shape, jnp.float32)
    if shards:
        array = array * levels(key, shape, shards, -0.22, 0.18)
    return jnp.clip(strengthened(array, jax.random.fold_in(key, 3), *heavy), -limit, limit).astype(held_as)


def setup_inputs(seed: int = 0, part: int = 0) -> dict:
    streams_of = jax.random.split(jax.random.key(seed), 5)
    part_splits = jax.random.split(jax.random.fold_in(streams_of[4], part), 5)
    return {
        "left_panel": gaussian_with(part_splits[0], (LEFT, SLAB), LEFT ** -0.5, 0.02734375, ((0, 16),), (0, 1, 16, 2.0), jnp.float32),
        "earlier": noise(part_splits[1], (LEFT, RHS), 1.0, 6.0, ((0, 16),), jnp.float32),
        "diag_block": draw_diag_block(jax.random.fold_in(jax.random.fold_in(streams_of[4], part), 71), part),
        "chosen": with_ends(jax.random.randint(part_splits[3], (RHS,), 0, SLAB), jax.random.fold_in(part_splits[3], 1), 0, SLAB - 1).astype(jnp.int32),
    }


def reference(left_panel, earlier, diag_block, chosen):
    coupled = jnp.dot(left_panel.T.astype(jnp.float32), earlier.astype(jnp.float32), precision=lax.Precision.HIGHEST, preferred_element_type=jnp.float32)
    slab_rows = jnp.arange(SLAB, dtype=jnp.int32)
    unit_cols = (slab_rows[:, None] == chosen[None, :]).astype(jnp.float32)
    right_side = unit_cols - coupled
    forward = lax.linalg.triangular_solve(diag_block, right_side, left_side=True, lower=True)
    marginal = lax.linalg.triangular_solve(diag_block, forward, left_side=True, lower=True, transpose_a=True)
    updated = earlier - jnp.dot(left_panel.astype(jnp.float32), marginal.astype(jnp.float32), precision=lax.Precision.HIGHEST, preferred_element_type=jnp.float32)
    return (marginal, updated)
```

```python
import functools

import jax
import jax.numpy as jnp
from jax import lax
from jax.experimental import pallas as pl
from jax.experimental.pallas import tpu as pltpu
from jax.sharding import PartitionSpec as P

F32 = jnp.float32
BF16 = jnp.bfloat16
NN = (((1,), (0,)), ((), ()))
NT = (((1,), (1,)), ((), ()))
TN = (((0,), (0,)), ((), ()))
VMEM_LIMIT = 60 * 2**20


def split(value):
    high = value.astype(BF16)
    return high, (value - high.astype(F32)).astype(BF16)


def mul(a, b, dims):
    return lax.dot_general(a, b, dims, preferred_element_type=F32)


def mul_parts(a, b, dims):
    return mul(a[0], b[0], dims) + (mul(a[0], b[1], dims) + mul(a[1], b[0], dims))


def bits_of(size):
    count = size.bit_length() - 1
    assert size == 1 << count
    return count


def tile_rows(rows, most):
    return max(t for t in range(8, most + 1, 8) if rows % t == 0)


def params(**more):
    return pltpu.CompilerParams(vmem_limit_bytes=VMEM_LIMIT, **more)


SMEM = pl.BlockSpec(memory_space=pltpu.SMEM)
VMEM = pl.BlockSpec(memory_space=pltpu.VMEM)
ANY = pl.BlockSpec(memory_space=pltpu.HBM)


def coupling_kernel(offset, opens, closes, extra, place_ref, left_ref, earlier_ref, first_ref, *refs):
    outs, total = refs[extra:-1], refs[-1]
    step = pl.program_id(0)
    cols, width = total.shape

    @pl.when(step == 0)
    def _():
        if opens:
            slab = lax.broadcasted_iota(jnp.int32, (cols, width), 1) + offset
            total[...] = jnp.where(first_ref[...] == slab, 1.0, 0.0)
        else:
            total[...] = first_ref[...]

    total[...] -= mul_parts(split(earlier_ref[...]), split(left_ref[...]), TN)

    @pl.when(step == pl.num_programs(0) - 1)
    def _():
        if closes:
            half = cols // 2
            mine = place_ref[0]
            outs[0][...] = total[pl.ds(pl.multiple_of(mine * half, 8), half), :]
            outs[1][...] = total[pl.ds(pl.multiple_of((1 - mine) * half, 8), half), :]
        else:
            outs[0][...] = total[...]


def coupling(name, first, width, steps, opens, closes, place, left, earlier, start, after):
    rows, cols = earlier.shape
    tile = tile_rows(rows, 1504)
    begin, end = steps
    column = first // width
    shape = (cols // 2, width) if closes else (cols, width)
    outs = 2 if closes else 1
    return pl.pallas_call(
        functools.partial(coupling_kernel, first, opens, closes, len(after)),
        grid=(end - begin,),
        in_specs=[
            SMEM,
            pl.BlockSpec((tile, width), lambda i: (i + begin, column)),
            pl.BlockSpec((tile, cols), lambda i: (i + begin, 0)),
            pl.BlockSpec(start.shape, lambda i: (0, 0)),
        ]
        + [ANY] * len(after),
        out_specs=[pl.BlockSpec(shape, lambda i: (0, 0))] * outs,
        out_shape=[jax.ShapeDtypeStruct(shape, F32)] * outs,
        scratch_shapes=[pltpu.VMEM((cols, width), F32)],
        compiler_params=params(),
        cost_estimate=pl.CostEstimate(
            flops=6 * (end - begin) * tile * width * cols,
            bytes_accessed=4 * (end - begin) * tile * (width + cols),
            transcendentals=0,
        ),
        name=name,
    )(place, left, earlier, start, *after)


def prepare_kernel(count, extra, place_ref, *refs):
    sources = refs[:count]
    panel_out, panel_high, panel_low, panel, sems = refs[count + extra :]
    size = sources[0].shape[1]
    copies = []
    for index, source in enumerate(sources):
        row = pl.multiple_of(place_ref[1 + 2 * index], 8)
        column = pl.multiple_of(place_ref[2 + 2 * index], 128)
        target = panel.at[pl.ds(row, source.shape[0]), pl.ds(column, size)]
        copies.append(pltpu.make_async_copy(source, target, sems.at[index]))
    for copy in copies:
        copy.start()
    for copy in copies:
        copy.wait()
    high, low = split(panel[...])
    panel_high[...] = high
    panel_low[...] = low
    for index in range(panel.shape[1] // size):
        row = pl.multiple_of(place_ref[0] + index * size, 8)
        panel_out[index * size : (index + 1) * size, :] = panel[pl.ds(row, size), index * size : (index + 1) * size]


def invert_kernel(block_ref, inv_high, inv_low):
    size = block_ref.shape[1]
    blocks = [block_ref[i : i + size, :] for i in range(0, block_ref.shape[0], size)]

    def exact(a, b, dims):
        return mul_parts(split(a), split(b), dims)

    small = min(128, size)
    exact = functools.partial(
        lax.dot_general, precision=lax.Precision.HIGHEST, preferred_element_type=F32
    )
    row = lax.broadcasted_iota(jnp.int32, (small, small), 0)
    col = lax.broadcasted_iota(jnp.int32, (small, small), 1)
    found = []
    tiles = []
    for start in range(0, len(blocks) * size, small):
        block, inside = blocks[start // size], start % size
        tile = block[inside : inside + small, inside : inside + small]
        tiles.append(tile)
        found.append(jnp.where(row == col, 1.0 / jnp.where(row == col, tile, 1.0), 0.0))
    reach = 1
    while reach < small:
        shift = bits_of(reach)
        below = ((row >> shift) == (col >> shift) + 1) & ((row >> (shift + 1)) == (col >> (shift + 1)))
        inner = [exact(jnp.where(below, t, 0.0), x, NN) for t, x in zip(tiles, found)]
        found = [x - exact(x, y, NN) for x, y in zip(found, inner)]
        reach *= 2
    while reach < size:
        merged = []
        for index in range(0, len(found), 2):
            first, second = found[index], found[index + 1]
            block, start = blocks[index * reach // size], index * reach % size
            corner = block[start + reach : start + 2 * reach, start : start + reach]
            lower = -exact(second, exact(corner, first, NN), NN)
            top = jnp.concatenate([first, jnp.zeros_like(first)], axis=1)
            merged.append(jnp.concatenate([top, jnp.concatenate([lower, second], axis=1)], axis=0))
        found = merged
        reach *= 2
    for index, value in enumerate(found):
        high, low = split(value)
        inv_high[index * size : (index + 1) * size, :] = high
        inv_low[index * size : (index + 1) * size, :] = low


def invert(blocks):
    return pl.pallas_call(
        invert_kernel,
        in_specs=[VMEM],
        out_specs=[VMEM] * 2,
        out_shape=[jax.ShapeDtypeStruct(blocks.shape, BF16)] * 2,
        compiler_params=params(),
        cost_estimate=pl.CostEstimate(
            flops=80 * blocks.shape[1] ** 2 * blocks.shape[0], bytes_accessed=8 * blocks.size, transcendentals=0
        ),
        name="invert",
    )(blocks)


def prepare(places, sources, shape, after):
    width = sources[0].shape[1]
    rows, span = shape
    return pl.pallas_call(
        functools.partial(prepare_kernel, len(sources), len(after)),
        in_specs=[SMEM] + [ANY] * (len(sources) + len(after)),
        out_specs=[VMEM] * 3,
        out_shape=[jax.ShapeDtypeStruct((span, width), F32)] + [jax.ShapeDtypeStruct(shape, BF16)] * 2,
        scratch_shapes=[pltpu.VMEM(shape, F32), pltpu.SemaphoreType.DMA((len(sources),))],
        compiler_params=params(),
        cost_estimate=pl.CostEstimate(
            flops=80 * width**2 * span, bytes_accessed=8 * span * (width + rows), transcendentals=0
        ),
        name="prepare",
    )(places, *sources, *after)


def sweep_kernel(side, forward, backward, terms, place_ref, *refs):
    added = refs[:terms]
    below_ref = refs[terms] if not side else None
    refs = refs[terms + (below_ref is not None) :]
    inv_high, inv_low, panel_high, panel_low = refs[:4]
    outs = refs[4:-4]
    invs, upper, lower, sems = refs[-4:]
    rows, span = outs[0].shape
    width = invs.shape[2]
    count = span // width
    far = not side

    @pl.when(place_ref[0] == side)
    def _():
        wanted = [(inv_high, invs.at[0]), (inv_low, invs.at[1])]
        wanted += [
            (panel_high.at[pl.ds(side * span, span), :], upper.at[0]),
            (panel_low.at[pl.ds(side * span, span), :], upper.at[1]),
        ]
        if far:
            wanted += [
                (panel_high.at[pl.ds(span, span), :], lower.at[0]),
                (panel_low.at[pl.ds(span, span), :], lower.at[1]),
            ]
        copies = [
            pltpu.make_async_copy(source, target, sems.at[index])
            for index, (source, target) in enumerate(wanted)
        ]
        order = [4, 5, 0, 1, 2, 3] if far and not forward else range(len(copies))
        for index in order:
            copies[index].start()

        def part(store, i, j):
            at = (slice(i * width, (i + 1) * width), slice(j * width, (j + 1) * width))
            return store[0, at[0], at[1]], store[1, at[0], at[1]]

        def inverse(i):
            at = slice(i * width, (i + 1) * width)
            return invs[0, at, :], invs[1, at, :]

        total = added[0][...]
        for ref in added[1:]:
            total = total + ref[...]
        waited = [False] * len(copies)

        def need(*which):
            for index in which:
                if not waited[index]:
                    copies[index].wait()
                    waited[index] = True

        values = [total[:, i * width : (i + 1) * width] for i in range(count)]
        if forward:
            need(0, 1)
            split_values = []
            for i in range(count):
                value = values[i]
                for j in range(i):
                    need(2, 3)
                    value = value - mul_parts(split_values[j], part(upper, i, j), NT)
                values[i] = mul_parts(split(value), inverse(i), NT)
                split_values.append(split(values[i]))
            if not backward:
                outs[0][...] = jnp.concatenate(values, axis=1)
                need(4, 5)
                whole = (
                    jnp.concatenate([v[0] for v in split_values], axis=1),
                    jnp.concatenate([v[1] for v in split_values], axis=1),
                )
                outs[1][...] = below_ref[...] - mul_parts(whole, (lower[0], lower[1]), NT)
        if backward:
            if not side:
                need(4, 5)
                taken = mul_parts(split(below_ref[...]), (lower[0], lower[1]), NN)
                values = [v - taken[:, i * width : (i + 1) * width] for i, v in enumerate(values)]
            need(0, 1)
            done = [None] * count
            for i in reversed(range(count)):
                value = values[i]
                for j in range(i + 1, count):
                    need(2, 3)
                    value = value - mul_parts(done[j], part(upper, j, i), NN)
                values[i] = mul_parts(split(value), inverse(i), NN)
                done[i] = split(values[i])
            outs[0][...] = jnp.concatenate(values, axis=1)
        need(*range(len(copies)))

    if backward:

        @pl.when(place_ref[0] != side)
        def _():
            outs[0][...] = jnp.zeros_like(outs[0])


def sweep(name, side, forward, backward, place, added, below, ready):
    shape = added[0].shape
    span = shape[1]
    width = ready[0].shape[1]
    below = [] if below is None else [below]
    outs = 2 if forward and not backward else 1
    far = 2 if not side else 1
    return pl.pallas_call(
        functools.partial(sweep_kernel, side, forward, backward, len(added)),
        in_specs=[SMEM] + [VMEM] * (len(added) + len(below)) + [ANY] * 4,
        out_specs=[VMEM] * outs,
        out_shape=[jax.ShapeDtypeStruct(shape, F32)] * outs,
        scratch_shapes=[
            pltpu.VMEM((2, span, width), BF16),
            pltpu.VMEM((2, span, span), BF16),
            pltpu.VMEM((2, span if far == 2 else 16, span), BF16),
            pltpu.SemaphoreType.DMA((6,)),
        ],
        compiler_params=params(),
        cost_estimate=pl.CostEstimate(
            flops=6 * 256 * span**2 * far, bytes_accessed=4 * span**2 * far, transcendentals=0
        ),
        name=name,
    )(place, *added, *below, *ready)


def gather_kernel(near, col_count, pair_count, place_ref, *refs):
    pieces = refs[:-4]
    rows_ref, high_ref, low_ref, whole = refs[-4:]
    piece = pieces[0].shape[0] // near
    for pair in range(pair_count):
        for col in range(col_count):
            source = pieces[pair * col_count + col]
            block = ((place_ref[0] ^ pair) * col_count + (place_ref[1] ^ col)) * near
            for plane in range(near):
                start = pl.multiple_of((block + (place_ref[3] ^ plane)) * piece, 8)
                whole[pl.ds(start, piece), :] = source[plane * piece : (plane + 1) * piece, :]
    kept = rows_ref.shape[0]
    rows_ref[...] = whole[pl.ds(pl.multiple_of(place_ref[2] * kept, 8), kept), :]
    high, low = split(whole[...].T)
    high_ref[...] = high
    low_ref[...] = low


def gathered(name, counts, place, pieces, kept, cols):
    span = pieces[0].shape[1]
    near, col_count, pair_count = counts
    if pieces[0].shape[0] // near % 8:
        order = place[3] ^ jnp.arange(near, dtype=jnp.int32)
        pieces = [jnp.take(v.reshape(near, -1, span), order, axis=0).reshape(v.shape) for v in pieces]
        place = place.at[3].set(0)
        near = 1
    return pl.pallas_call(
        functools.partial(gather_kernel, near, col_count, pair_count),
        in_specs=[SMEM] + [VMEM] * len(pieces),
        out_specs=[VMEM] * 3,
        out_shape=[
            jax.ShapeDtypeStruct((kept, span), F32),
            jax.ShapeDtypeStruct((span, cols), BF16),
            jax.ShapeDtypeStruct((span, cols), BF16),
        ],
        scratch_shapes=[pltpu.VMEM((cols, span), F32)],
        compiler_params=params(),
        cost_estimate=pl.CostEstimate(
            flops=cols * span, bytes_accessed=8 * cols * span, transcendentals=0
        ),
        name=name,
    )(place, *pieces)


def update_kernel(before_ref, left_ref, high_ref, low_ref, *refs):
    product = mul_parts(split(left_ref[...]), (high_ref[...], low_ref[...]), NN)
    refs[-1][...] = before_ref[...] - product


def update(name, first, steps, tile, before, left, high, low, into, after):
    rows, cols = before.shape
    span = high.shape[0]
    column = first // span
    begin, end = steps
    extra = ([] if into is None else [into]) + list(after)
    return pl.pallas_call(
        update_kernel,
        grid=(end - begin,),
        in_specs=[
            pl.BlockSpec((tile, cols), lambda i: (i + begin, 0)),
            pl.BlockSpec((tile, span), lambda i: (i + begin, column)),
            pl.BlockSpec((span, cols), lambda i: (0, 0)),
            pl.BlockSpec((span, cols), lambda i: (0, 0)),
        ]
        + [ANY] * len(extra),
        out_specs=pl.BlockSpec((tile, cols), lambda i: (i + begin, 0)),
        out_shape=jax.ShapeDtypeStruct((rows, cols), F32),
        input_output_aliases={} if into is None else {4: 0},
        compiler_params=params(),
        cost_estimate=pl.CostEstimate(
            flops=6 * (end - begin) * tile * span * cols,
            bytes_accessed=4 * (end - begin) * tile * (span + 2 * cols),
            transcendentals=0,
        ),
        name=name,
    )(before, left, high, low, *extra)


def swapped(value, axis, distance, size):
    return lax.ppermute(value, axis, [(i, i ^ distance) for i in range(size)])


def parted(value, bit, axis):
    half = value.shape[0] // 2
    mine = (lax.axis_index(axis) >> bit) & 1
    kept = lax.dynamic_slice_in_dim(value, mine * half, half, 0)
    sent = lax.dynamic_slice_in_dim(value, (1 - mine) * half, half, 0)
    return kept, sent


def local(left_panel, earlier, diag_block, chosen):
    planes = lax.axis_size("row")
    col_count = lax.axis_size("col")
    pair_count = lax.axis_size("rep")
    assert pair_count == 2
    near = planes // 2
    plane = lax.axis_index("row").astype(jnp.int32)
    col = lax.axis_index("col").astype(jnp.int32)
    pair = lax.axis_index("rep").astype(jnp.int32)
    height, width = diag_block.shape
    slab = left_panel.shape[1]
    span = slab // 2
    rows, cols = earlier.shape
    own = chosen.shape[0]
    slot = plane * pair_count + pair
    side = plane // near
    inner = plane % near
    side_at = side.reshape(1)
    pair_at = pair.reshape(1)
    place = jnp.stack([pair, col, slot, inner])

    share = height // pair_count
    mine = lax.dynamic_slice_in_dim(diag_block, pair * share, share, 0)
    beside = [mine] + [swapped(mine, "col", far, col_count) for far in range(1, col_count)]
    above = [None] + [swapped(mine, "row", up, planes) for up in range(1, near)]
    sources = [diag_block]
    starts = [side * span, col * height, inner * width]
    for up in range(near):
        for far in range(col_count):
            if up or far:
                if up and far:
                    part = swapped(beside[far], "row", up, planes)
                else:
                    part = above[up] if up else beside[far]
                sources += [part, swapped(part, "rep", 1, pair_count)]
                block = (col ^ far) * height
                column = (inner ^ up) * width
                starts += [block + pair * share, column, block + (1 - pair) * share, column]

    marks = jnp.full((cols, 1), -1, jnp.int32)
    entries = jnp.where(col == 0, chosen, -1).reshape(own, 1)
    marks = lax.dynamic_update_slice(marks, entries, (slot * own, 0))

    tiles = rows // tile_rows(rows, 1504)
    middle = tiles // 2

    def over_pair(parts):
        return parts[0] + swapped(parts[1], "rep", 1, pair_count)

    def over(value, axis, size, count):
        for bit in reversed(range(bits_of(count))):
            kept, sent = parted(value, bit, axis)
            value = kept + swapped(sent, axis, 1 << bit, size)
        return value

    def crossed(value, target):
        pairs = [(i, i ^ near) for i in range(planes) if i // near != target]
        return lax.ppermute(value, "row", pairs)

    low = coupling("coupling_low", 0, span, (0, tiles), True, True, pair_at, left_panel, earlier, marks, [])
    low_rep = over_pair(low)
    low_col = over(low_rep, "col", col_count, col_count)
    if middle:
        (begun,) = coupling(
            "coupling_high_a", span, span, (0, middle), True, False, pair_at, left_panel, earlier, marks,
            [low[0]] + beside[1:] + above[1:],
        )
        high = coupling(
            "coupling_high_b", span, span, (middle, tiles), False, True, pair_at, left_panel, earlier, begun,
            [low_rep],
        )
    else:
        high = coupling("coupling_high", span, span, (0, tiles), True, True, pair_at, left_panel, earlier, marks, [])
    high_rep = over_pair(high)
    low_near = over(low_col, "row", planes, near)
    blocks, *panel = prepare(jnp.stack(starts), sources, (slab, near * width), [high[0], low_col])
    low_side = [low_near, crossed(low_near, 0)]
    ready = [*invert(blocks), *panel]
    high_near = over(over(high_rep, "col", col_count, col_count), "row", planes, near)

    solved, sent = sweep("forward_low", 0, True, False, side_at, low_side, high_near, ready)
    (second,) = sweep("both_high", 1, True, True, side_at, [high_near, crossed(sent, 1)], None, ready)
    second_low = crossed(second, 0)
    (first,) = sweep("backward_low", 0, False, True, side_at, [solved], second_low, ready)

    def pieces_of(value):
        stack = [value] + [swapped(value, "row", up, planes) for up in range(1, near)]
        return jnp.concatenate(stack, axis=0)

    def over_cols(stack):
        return [stack] + [swapped(stack, "col", far, col_count) for far in range(1, col_count)]

    def over_pairs(across):
        return across + [swapped(part, "rep", 1, pair_count) for part in across]

    counts = (near, col_count, pair_count)
    tile = tile_rows(rows, 752)
    tiles = rows // tile
    cuts = [0, 3 * tiles // 8, 6 * tiles // 8, tiles]
    high_pieces = over_pairs(over_cols(pieces_of(second + second_low)))
    rows_high, high_a, high_b = gathered("gathered_high", counts, place, high_pieces, own, cols)
    whole_first = first + crossed(first, 1)
    stack_first = pieces_of(whole_first)
    across_first = over_cols(stack_first)
    waits = [[first, whole_first], [stack_first], across_first[1:]]
    partial = None
    for index in range(3):
        steps = (cuts[index], cuts[index + 1])
        if steps[0] < steps[1]:
            partial = update(
                f"update_high_{index}", span, steps, tile, earlier, left_panel, high_a, high_b, partial, waits[index]
            )
    rows_low, low_a, low_b = gathered("gathered_low", counts, place, over_pairs(across_first), own, cols)
    tile = tile_rows(rows, 1504)
    updated = update("update_low", 0, (0, rows // tile), tile, partial, left_panel, low_a, low_b, None, [])
    whole = jnp.concatenate([rows_low, rows_high], axis=1)
    marginal = lax.dynamic_slice_in_dim(whole, col * height, height, 1).T
    return (marginal, updated)


def solution(mesh):
    placed = (
        P(("groups", "row", "col", "rep"), None),
        P(("groups", "row", "col", "rep"), None),
        P(("groups", "col"), "row"),
        P(("groups", "row", "rep")),
    )
    return jax.shard_map(
        local,
        mesh=mesh,
        in_specs=placed,
        out_specs=(P(("groups", "col"), ("row", "rep")), P(("groups", "row", "col", "rep"), None)),
        check_vma=False,
    )
```

```python
import functools

import jax
import jax.numpy as jnp
from jax import lax
from jax.experimental import pallas as pl
from jax.experimental.pallas import tpu as pltpu
from jax.sharding import PartitionSpec as P

F32 = jnp.float32
BF16 = jnp.bfloat16
NN = (((1,), (0,)), ((), ()))
NT = (((1,), (1,)), ((), ()))
TN = (((0,), (0,)), ((), ()))
VMEM_LIMIT = 60 * 2**20


def split(value):
    high = value.astype(BF16)
    return high, (value - high.astype(F32)).astype(BF16)


def mul(a, b, dims):
    return lax.dot_general(a, b, dims, preferred_element_type=F32)


def mul_parts(a, b, dims):
    return mul(a[0], b[0], dims) + (mul(a[0], b[1], dims) + mul(a[1], b[0], dims))


def bits_of(size):
    count = size.bit_length() - 1
    assert size == 1 << count
    return count


def tile_rows(rows, most):
    return max(t for t in range(8, most + 1, 8) if rows % t == 0)


def params(**more):
    return pltpu.CompilerParams(vmem_limit_bytes=VMEM_LIMIT, **more)


SMEM = pl.BlockSpec(memory_space=pltpu.SMEM)
VMEM = pl.BlockSpec(memory_space=pltpu.VMEM)
ANY = pl.BlockSpec(memory_space=pltpu.HBM)


def coupling_kernel(offset, opens, closes, extra, place_ref, left_ref, earlier_ref, first_ref, *refs):
    outs, total = refs[extra:-1], refs[-1]
    step = pl.program_id(0)
    cols, width = total.shape

    @pl.when(step == 0)
    def _():
        if opens:
            slab = lax.broadcasted_iota(jnp.int32, (cols, width), 1) + offset
            total[...] = jnp.where(first_ref[...] == slab, 1.0, 0.0)
        else:
            total[...] = first_ref[...]

    total[...] -= mul_parts(split(earlier_ref[...]), split(left_ref[...]), TN)

    @pl.when(step == pl.num_programs(0) - 1)
    def _():
        if closes:
            half = cols // 2
            mine = place_ref[0]
            outs[0][...] = total[pl.ds(pl.multiple_of(mine * half, 8), half), :]
            outs[1][...] = total[pl.ds(pl.multiple_of((1 - mine) * half, 8), half), :]
        else:
            outs[0][...] = total[...]


def coupling(name, first, width, steps, opens, closes, place, left, earlier, start, after):
    rows, cols = earlier.shape
    tile = tile_rows(rows, 1504)
    begin, end = steps
    column = first // width
    shape = (cols // 2, width) if closes else (cols, width)
    outs = 2 if closes else 1
    return pl.pallas_call(
        functools.partial(coupling_kernel, first, opens, closes, len(after)),
        grid=(end - begin,),
        in_specs=[
            SMEM,
            pl.BlockSpec((tile, width), lambda i: (i + begin, column)),
            pl.BlockSpec((tile, cols), lambda i: (i + begin, 0)),
            pl.BlockSpec(start.shape, lambda i: (0, 0)),
        ]
        + [ANY] * len(after),
        out_specs=[pl.BlockSpec(shape, lambda i: (0, 0))] * outs,
        out_shape=[jax.ShapeDtypeStruct(shape, F32)] * outs,
        scratch_shapes=[pltpu.VMEM((cols, width), F32)],
        compiler_params=params(),
        cost_estimate=pl.CostEstimate(
            flops=6 * (end - begin) * tile * width * cols,
            bytes_accessed=4 * (end - begin) * tile * (width + cols),
            transcendentals=0,
        ),
        name=name,
    )(place, left, earlier, start, *after)


def prepare_kernel(count, extra, place_ref, *refs):
    sources = refs[:count]
    inv_high, inv_low, panel_high, panel_low, panel, sems = refs[count + extra :]
    size = sources[0].shape[1]
    copies = []
    for index, source in enumerate(sources):
        row = pl.multiple_of(place_ref[1 + 2 * index], 8)
        column = pl.multiple_of(place_ref[2 + 2 * index], 128)
        target = panel.at[pl.ds(row, source.shape[0]), pl.ds(column, size)]
        copies.append(pltpu.make_async_copy(source, target, sems.at[index]))
    for copy in copies:
        copy.start()
    for copy in copies:
        copy.wait()
    high, low = split(panel[...])
    panel_high[...] = high
    panel_low[...] = low
    blocks = []
    for index in range(panel.shape[1] // size):
        row = pl.multiple_of(place_ref[0] + index * size, 8)
        blocks.append(panel[pl.ds(row, size), index * size : (index + 1) * size])

    def exact(a, b, dims):
        return mul_parts(split(a), split(b), dims)

    small = min(128, size)
    row = lax.broadcasted_iota(jnp.int32, (small, small), 0)
    col = lax.broadcasted_iota(jnp.int32, (small, small), 1)
    found = []
    tiles = []
    for start in range(0, len(blocks) * size, small):
        block, inside = blocks[start // size], start % size
        tile = block[inside : inside + small, inside : inside + small]
        tiles.append(tile)
        found.append(jnp.where(row == col, 1.0 / jnp.where(row == col, tile, 1.0), 0.0))
    reach = 1
    while reach < small:
        shift = bits_of(reach)
        below = ((row >> shift) == (col >> shift) + 1) & ((row >> (shift + 1)) == (col >> (shift + 1)))
        inner = [exact(jnp.where(below, t, 0.0), x, NN) for t, x in zip(tiles, found)]
        found = [x - exact(x, y, NN) for x, y in zip(found, inner)]
        reach *= 2
    while reach < size:
        merged = []
        for index in range(0, len(found), 2):
            first, second = found[index], found[index + 1]
            block, start = blocks[index * reach // size], index * reach % size
            corner = block[start + reach : start + 2 * reach, start : start + reach]
            lower = -exact(second, exact(corner, first, NN), NN)
            top = jnp.concatenate([first, jnp.zeros_like(first)], axis=1)
            merged.append(jnp.concatenate([top, jnp.concatenate([lower, second], axis=1)], axis=0))
        found = merged
        reach *= 2
    for index, value in enumerate(found):
        high, low = split(value)
        inv_high[index * size : (index + 1) * size, :] = high
        inv_low[index * size : (index + 1) * size, :] = low


def prepare(places, sources, shape, after):
    width = sources[0].shape[1]
    rows, span = shape
    return pl.pallas_call(
        functools.partial(prepare_kernel, len(sources), len(after)),
        in_specs=[SMEM] + [ANY] * (len(sources) + len(after)),
        out_specs=[VMEM] * 4,
        out_shape=[jax.ShapeDtypeStruct((span, width), BF16)] * 2 + [jax.ShapeDtypeStruct(shape, BF16)] * 2,
        scratch_shapes=[pltpu.VMEM(shape, F32), pltpu.SemaphoreType.DMA((len(sources),))],
        compiler_params=params(),
        cost_estimate=pl.CostEstimate(
            flops=80 * width**2 * span, bytes_accessed=8 * span * (width + rows), transcendentals=0
        ),
        name="prepare",
    )(places, *sources, *after)


def sweep_kernel(side, forward, backward, terms, place_ref, *refs):
    added = refs[:terms]
    below_ref = refs[terms] if not side else None
    refs = refs[terms + (below_ref is not None) :]
    inv_high, inv_low, panel_high, panel_low = refs[:4]
    outs = refs[4:-4]
    invs, upper, lower, sems = refs[-4:]
    rows, span = outs[0].shape
    width = invs.shape[2]
    count = span // width
    far = not side

    @pl.when(place_ref[0] == side)
    def _():
        wanted = [(inv_high, invs.at[0]), (inv_low, invs.at[1])]
        wanted += [
            (panel_high.at[pl.ds(side * span, span), :], upper.at[0]),
            (panel_low.at[pl.ds(side * span, span), :], upper.at[1]),
        ]
        if far:
            wanted += [
                (panel_high.at[pl.ds(span, span), :], lower.at[0]),
                (panel_low.at[pl.ds(span, span), :], lower.at[1]),
            ]
        copies = [
            pltpu.make_async_copy(source, target, sems.at[index])
            for index, (source, target) in enumerate(wanted)
        ]
        order = [4, 5, 0, 1, 2, 3] if far and not forward else range(len(copies))
        for index in order:
            copies[index].start()

        def part(store, i, j):
            at = (slice(i * width, (i + 1) * width), slice(j * width, (j + 1) * width))
            return store[0, at[0], at[1]], store[1, at[0], at[1]]

        def inverse(i):
            at = slice(i * width, (i + 1) * width)
            return invs[0, at, :], invs[1, at, :]

        total = added[0][...]
        for ref in added[1:]:
            total = total + ref[...]
        waited = [False] * len(copies)

        def need(*which):
            for index in which:
                if not waited[index]:
                    copies[index].wait()
                    waited[index] = True

        values = [total[:, i * width : (i + 1) * width] for i in range(count)]
        if forward:
            need(0, 1)
            split_values = []
            for i in range(count):
                value = values[i]
                for j in range(i):
                    need(2, 3)
                    value = value - mul_parts(split_values[j], part(upper, i, j), NT)
                values[i] = mul_parts(split(value), inverse(i), NT)
                split_values.append(split(values[i]))
            if not backward:
                outs[0][...] = jnp.concatenate(values, axis=1)
                need(4, 5)
                whole = (
                    jnp.concatenate([v[0] for v in split_values], axis=1),
                    jnp.concatenate([v[1] for v in split_values], axis=1),
                )
                outs[1][...] = below_ref[...] - mul_parts(whole, (lower[0], lower[1]), NT)
        if backward:
            if not side:
                need(4, 5)
                taken = mul_parts(split(below_ref[...]), (lower[0], lower[1]), NN)
                values = [v - taken[:, i * width : (i + 1) * width] for i, v in enumerate(values)]
            need(0, 1)
            done = [None] * count
            for i in reversed(range(count)):
                value = values[i]
                for j in range(i + 1, count):
                    need(2, 3)
                    value = value - mul_parts(done[j], part(upper, j, i), NN)
                values[i] = mul_parts(split(value), inverse(i), NN)
                done[i] = split(values[i])
            outs[0][...] = jnp.concatenate(values, axis=1)
        need(*range(len(copies)))

    if backward:

        @pl.when(place_ref[0] != side)
        def _():
            outs[0][...] = jnp.zeros_like(outs[0])


def sweep(name, side, forward, backward, place, added, below, ready):
    shape = added[0].shape
    span = shape[1]
    width = ready[0].shape[1]
    below = [] if below is None else [below]
    outs = 2 if forward and not backward else 1
    far = 2 if not side else 1
    return pl.pallas_call(
        functools.partial(sweep_kernel, side, forward, backward, len(added)),
        in_specs=[SMEM] + [VMEM] * (len(added) + len(below)) + [ANY] * 4,
        out_specs=[VMEM] * outs,
        out_shape=[jax.ShapeDtypeStruct(shape, F32)] * outs,
        scratch_shapes=[
            pltpu.VMEM((2, span, width), BF16),
            pltpu.VMEM((2, span, span), BF16),
            pltpu.VMEM((2, span if far == 2 else 16, span), BF16),
            pltpu.SemaphoreType.DMA((6,)),
        ],
        compiler_params=params(),
        cost_estimate=pl.CostEstimate(
            flops=6 * 256 * span**2 * far, bytes_accessed=4 * span**2 * far, transcendentals=0
        ),
        name=name,
    )(place, *added, *below, *ready)


def gather_kernel(near, col_count, pair_count, place_ref, *refs):
    pieces = refs[:-4]
    rows_ref, high_ref, low_ref, whole = refs[-4:]
    piece = pieces[0].shape[0] // near
    for pair in range(pair_count):
        for col in range(col_count):
            source = pieces[pair * col_count + col]
            block = ((place_ref[0] ^ pair) * col_count + (place_ref[1] ^ col)) * near
            for plane in range(near):
                start = pl.multiple_of((block + (place_ref[3] ^ plane)) * piece, 8)
                whole[pl.ds(start, piece), :] = source[plane * piece : (plane + 1) * piece, :]
    kept = rows_ref.shape[0]
    rows_ref[...] = whole[pl.ds(pl.multiple_of(place_ref[2] * kept, 8), kept), :]
    high, low = split(whole[...].T)
    high_ref[...] = high
    low_ref[...] = low


def gathered(name, counts, place, pieces, kept, cols):
    span = pieces[0].shape[1]
    near, col_count, pair_count = counts
    if pieces[0].shape[0] // near % 8:
        order = place[3] ^ jnp.arange(near, dtype=jnp.int32)
        pieces = [jnp.take(v.reshape(near, -1, span), order, axis=0).reshape(v.shape) for v in pieces]
        place = place.at[3].set(0)
        near = 1
    return pl.pallas_call(
        functools.partial(gather_kernel, near, col_count, pair_count),
        in_specs=[SMEM] + [VMEM] * len(pieces),
        out_specs=[VMEM] * 3,
        out_shape=[
            jax.ShapeDtypeStruct((kept, span), F32),
            jax.ShapeDtypeStruct((span, cols), BF16),
            jax.ShapeDtypeStruct((span, cols), BF16),
        ],
        scratch_shapes=[pltpu.VMEM((cols, span), F32)],
        compiler_params=params(),
        cost_estimate=pl.CostEstimate(
            flops=cols * span, bytes_accessed=8 * cols * span, transcendentals=0
        ),
        name=name,
    )(place, *pieces)


def update_kernel(before_ref, left_ref, high_ref, low_ref, *refs):
    product = mul_parts(split(left_ref[...]), (high_ref[...], low_ref[...]), NN)
    refs[-1][...] = before_ref[...] - product


def update(name, first, steps, tile, before, left, high, low, into, after):
    rows, cols = before.shape
    span = high.shape[0]
    column = first // span
    begin, end = steps
    extra = ([] if into is None else [into]) + list(after)
    return pl.pallas_call(
        update_kernel,
        grid=(end - begin,),
        in_specs=[
            pl.BlockSpec((tile, cols), lambda i: (i + begin, 0)),
            pl.BlockSpec((tile, span), lambda i: (i + begin, column)),
            pl.BlockSpec((span, cols), lambda i: (0, 0)),
            pl.BlockSpec((span, cols), lambda i: (0, 0)),
        ]
        + [ANY] * len(extra),
        out_specs=pl.BlockSpec((tile, cols), lambda i: (i + begin, 0)),
        out_shape=jax.ShapeDtypeStruct((rows, cols), F32),
        input_output_aliases={} if into is None else {4: 0},
        compiler_params=params(),
        cost_estimate=pl.CostEstimate(
            flops=6 * (end - begin) * tile * span * cols,
            bytes_accessed=4 * (end - begin) * tile * (span + 2 * cols),
            transcendentals=0,
        ),
        name=name,
    )(before, left, high, low, *extra)


def swapped(value, axis, distance, size):
    return lax.ppermute(value, axis, [(i, i ^ distance) for i in range(size)])


def parted(value, bit, axis):
    half = value.shape[0] // 2
    mine = (lax.axis_index(axis) >> bit) & 1
    kept = lax.dynamic_slice_in_dim(value, mine * half, half, 0)
    sent = lax.dynamic_slice_in_dim(value, (1 - mine) * half, half, 0)
    return kept, sent


def local(left_panel, earlier, diag_block, chosen):
    planes = lax.axis_size("row")
    col_count = lax.axis_size("col")
    pair_count = lax.axis_size("rep")
    assert pair_count == 2
    near = planes // 2
    plane = lax.axis_index("row").astype(jnp.int32)
    col = lax.axis_index("col").astype(jnp.int32)
    pair = lax.axis_index("rep").astype(jnp.int32)
    height, width = diag_block.shape
    slab = left_panel.shape[1]
    span = slab // 2
    rows, cols = earlier.shape
    own = chosen.shape[0]
    slot = plane * pair_count + pair
    side = plane // near
    inner = plane % near
    side_at = side.reshape(1)
    pair_at = pair.reshape(1)
    place = jnp.stack([pair, col, slot, inner])

    share = height // pair_count
    mine = lax.dynamic_slice_in_dim(diag_block, pair * share, share, 0)
    beside = [mine] + [swapped(mine, "col", far, col_count) for far in range(1, col_count)]
    above = [None] + [swapped(mine, "row", up, planes) for up in range(1, near)]
    sources = [diag_block]
    starts = [side * span, col * height, inner * width]
    for up in range(near):
        for far in range(col_count):
            if up or far:
                if up and far:
                    part = swapped(beside[far], "row", up, planes)
                else:
                    part = above[up] if up else beside[far]
                sources += [part, swapped(part, "rep", 1, pair_count)]
                block = (col ^ far) * height
                column = (inner ^ up) * width
                starts += [block + pair * share, column, block + (1 - pair) * share, column]

    marks = jnp.full((cols, 1), -1, jnp.int32)
    entries = jnp.where(col == 0, chosen, -1).reshape(own, 1)
    marks = lax.dynamic_update_slice(marks, entries, (slot * own, 0))

    tiles = rows // tile_rows(rows, 1504)

    def over_pair(parts):
        return parts[0] + swapped(parts[1], "rep", 1, pair_count)

    def over(value, axis, size, count):
        for bit in reversed(range(bits_of(count))):
            kept, sent = parted(value, bit, axis)
            value = kept + swapped(sent, axis, 1 << bit, size)
        return value

    def crossed(value, target):
        pairs = [(i, i ^ near) for i in range(planes) if i // near != target]
        return lax.ppermute(value, "row", pairs)

    low = coupling("coupling_low", 0, span, (0, tiles), True, True, pair_at, left_panel, earlier, marks, [])
    low_rep = over_pair(low)
    low_col = over(low_rep, "col", col_count, col_count)
    high = coupling(
        "coupling_high", span, span, (0, tiles), True, True, pair_at, left_panel, earlier, marks,
        [low_rep] + beside[1:] + above[1:],
    )
    high_rep = over_pair(high)
    low_near = over(low_col, "row", planes, near)
    ready = prepare(jnp.stack(starts), sources, (slab, near * width), [high[0], low_col])
    low_side = [low_near, crossed(low_near, 0)]
    high_near = over(over(high_rep, "col", col_count, col_count), "row", planes, near)

    solved, sent = sweep("forward_low", 0, True, False, side_at, low_side, high_near, ready)
    (second,) = sweep("both_high", 1, True, True, side_at, [high_near, crossed(sent, 1)], None, ready)
    second_low = crossed(second, 0)
    (first,) = sweep("backward_low", 0, False, True, side_at, [solved], second_low, ready)

    def pieces_of(value):
        stack = [value] + [swapped(value, "row", up, planes) for up in range(1, near)]
        return jnp.concatenate(stack, axis=0)

    def over_cols(stack):
        return [stack] + [swapped(stack, "col", far, col_count) for far in range(1, col_count)]

    def over_pairs(across):
        return across + [swapped(part, "rep", 1, pair_count) for part in across]

    counts = (near, col_count, pair_count)
    tile = tile_rows(rows, 1504)
    tiles = rows // tile
    cuts = [0, tiles // 2, tiles]
    high_pieces = over_pairs(over_cols(pieces_of(second + second_low)))
    rows_high, high_a, high_b = gathered("gathered_high", counts, place, high_pieces, own, cols)
    whole_first = first + crossed(first, 1)
    stack_first = pieces_of(whole_first)
    across_first = over_cols(stack_first)
    waits = [[stack_first], across_first[1:]]
    partial = None
    for index in range(2):
        steps = (cuts[index], cuts[index + 1])
        if steps[0] < steps[1]:
            partial = update(
                f"update_high_{index}", span, steps, tile, earlier, left_panel, high_a, high_b, partial, waits[index]
            )
    rows_low, low_a, low_b = gathered("gathered_low", counts, place, over_pairs(across_first), own, cols)
    updated = update("update_low", 0, (0, tiles), tile, partial, left_panel, low_a, low_b, None, [])
    whole = jnp.concatenate([rows_low, rows_high], axis=1)
    marginal = lax.dynamic_slice_in_dim(whole, col * height, height, 1).T
    return (marginal, updated)


def solution(mesh):
    placed = (
        P(("groups", "row", "col", "rep"), None),
        P(("groups", "row", "col", "rep"), None),
        P(("groups", "col"), "row"),
        P(("groups", "row", "rep")),
    )
    return jax.shard_map(
        local,
        mesh=mesh,
        in_specs=placed,
        out_specs=(P(("groups", "col"), ("row", "rep")), P(("groups", "row", "col", "rep"), None)),
        check_vma=False,
    )
```
